32 devices in a mesh: wide: 8 (over z, y), mp: 4 (over x, core).
Axes of the slice: x: 2, y: 2, z: 4, core: 2. Of those that a mesh axis runs over, the one named last changes fastest.
Arguments:
- clip_feats: bfloat16 [1024, 768], P('wide'), may hold values from -6 to 6
- teacher_audio: bfloat16 [1024, 512], P('wide'), may hold values from -16 to 16
- teacher_text: bfloat16 [1024, 512], P(('wide', 'mp')), may hold values from -16 to 16
- w_first: bfloat16 [768, 512], P(None, 'mp'), may hold values from -0.21875 to 0.21875
- w_second: bfloat16 [512, 512], P('mp'), may hold values from -0.25 to 0.25
- pairing: int32 [1024], P('wide'), may hold values from 0 to 1023
Outputs:
- loss: float32 [], replicated
- grad_first: float32 [768, 512], P(None, 'mp')
- grad_second: float32 [512, 512], P('mp')
The draws below stay inside these ranges and needn't reach their ends.
All inputs are finite; a program needn't handle non-finite values.
Results may differ from the reference program's by a relative error of at most 0.0052.
Values may be sent and summed in bfloat16 or wider, within the bound.
No kernel may reach another device: no remote copies, remote signals or barrier semaphores. Data moves between devices by JAX's collectives and lax.ppermute only.
A program may use at most 64 MiB of HBM per device.

```python
import math
import jax
import jax.numpy as jnp
from jax import lax

D_AUDIO = 768
HIDDEN_UNITS = 512
EMBED = 512
ROWS_DEV = 128
BATCH = 1024


def unit_rows(values):
    return values / jnp.sqrt(jnp.sum(values * values, axis=1, keepdims=True))


def pair_index(key):
    return jax.random.randint(jax.random.fold_in(key, 11), (BATCH,), 0, BATCH, dtype=jnp.int32)


def caption_directions(key):
    groups = max(2, BATCH // 256)
    member = jax.random.randint(jax.random.fold_in(key, 12), (BATCH,), 0, groups, dtype=jnp.int32)
    centers = unit_rows(jax.random.normal(jax.random.fold_in(key, 13), (groups, EMBED), jnp.float32))
    pull = jax.random.uniform(jax.random.fold_in(key, 15), (groups,), jnp.float32, 0.55, 0.9)
    noise = unit_rows(jax.random.normal(jax.random.fold_in(key, 16), (BATCH, EMBED), jnp.float32))
    own_center = jnp.take(centers, member, axis=0)
    own_pull = jnp.take(pull, member, axis=0)[:, None]
    mixed = own_pull * own_center + jnp.sqrt(1.0 - own_pull * own_pull) * noise
    return unit_rows(mixed)


def row_scales(key, scale_low, scale_high):
    return jnp.exp(jax.random.uniform(key, (BATCH, 1), jnp.float32, math.log(scale_low), math.log(scale_high)))


def draw_pairing(key, part):
    return pair_index(key)


def draw_teacher_text(key, part):
    scale_low = 0.3
    scale_high = 3.0
    directions = caption_directions(key)
    scales = row_scales(jax.random.fold_in(key, 31), scale_low, scale_high)
    return jnp.clip(directions * scales * math.sqrt(float(EMBED)), -16.0, 16.0).astype(jnp.bfloat16)


def draw_teacher_audio(key, part):
    align_low = 0.3
    align_high = 0.9
    scale_low = 0.3
    scale_high = 3.0
    directions = caption_directions(key)
    paired = jnp.take(directions, pair_index(key), axis=0)
    align = jnp.exp(jax.random.uniform(jax.random.fold_in(key, 41), (BATCH, 1), jnp.float32, math.log(align_low), math.log(align_high)))
    noise = unit_rows(jax.random.normal(jax.random.fold_in(key, 42), (BATCH, EMBED), jnp.float32))
    mixed = unit_rows(align * paired + jnp.sqrt(1.0 - align * align) * noise)
    scales = row_scales(jax.random.fold_in(key, 43), scale_low, scale_high)
    return jnp.clip(mixed * scales * math.sqrt(float(EMBED)), -16.0, 16.0).astype(jnp.bfloat16)


def shard_levels(own_key, shape, split, low, top_value):
    def one(axis_at, blocks):
        draws = jax.random.uniform(jax.random.fold_in(jax.random.fold_in(own_key, 6), axis_at), (blocks,), jnp.float32, low / len(split), top_value / len(split))
        return jnp.repeat(jnp.exp(draws), shape[axis_at] // blocks).reshape((-1,) + (1,) * (len(shape) - axis_at - 1))

    gain = one(*split[0])
    for cut in split[1:]:
        gain = gain * one(*cut)
    return gain


def gaussian(stream_key, extent, scale, limit, split=(), kind=jnp.bfloat16):
    level = shard_levels(stream_key, extent, split, -0.22, 0.18) if split else 1.0
    drawn = jax.random.normal(stream_key, extent, jnp.float32) * scale * level
    return jnp.minimum(jnp.maximum(drawn, -limit), limit).astype(kind)


def setup_inputs(seed: int = 0) -> dict:
    key_list = jax.random.split(jax.random.key(seed), 7)
    clip_feats = gaussian(key_list[0], (BATCH, D_AUDIO), 1.0, 6.0, ((0, 8),))
    teacher_audio = draw_teacher_audio(jax.random.fold_in(key_list[6], 71), 0)
    teacher_text = draw_teacher_text(jax.random.fold_in(key_list[6], 71), 0)
    w_first = gaussian(key_list[3], (D_AUDIO, HIDDEN_UNITS), D_AUDIO ** -0.5, 0.21875, ((1, 4),))
    w_second = gaussian(key_list[4], (HIDDEN_UNITS, EMBED), HIDDEN_UNITS ** -0.5, 0.25, ((0, 4),))
    pairing = draw_pairing(jax.random.fold_in(key_list[6], 71), 0)
    return dict(clip_feats=clip_feats, teacher_audio=teacher_audio, teacher_text=teacher_text, w_first=w_first, w_second=w_second, pairing=pairing)


teacher_scale = 14.0
student_scale = 64.0
eps = 1e-06

def normalize(values):
    return values / jnp.sqrt(lax.optimization_barrier(jnp.sum(values * values, axis=1, keepdims=True)) + eps)

def inner_rows(left, right):
    return lax.dot_general(left, right, (((1,), (1,)), ((), ())), preferred_element_type=jnp.float32)

def reference(clip_feats, teacher_audio, teacher_text, w_first, w_second, pairing):
    total = clip_feats.shape[0]
    pre_act = jnp.dot(clip_feats, w_first, preferred_element_type=jnp.float32)
    gelu_out, gelu_back = jax.vjp(lambda u: jax.nn.gelu(u, approximate=False), pre_act)
    hidden = gelu_out.astype(jnp.bfloat16)
    raw = jnp.dot(hidden, w_second, preferred_element_type=jnp.float32)
    norm = jnp.sqrt(lax.optimization_barrier(jnp.sum(raw * raw, axis=1, keepdims=True)) + eps)
    student = raw / norm
    stud_b = student.astype(jnp.bfloat16)
    teach_b = normalize(teacher_audio.astype(jnp.float32)).astype(jnp.bfloat16)
    capt_b = normalize(teacher_text.astype(jnp.float32)).astype(jnp.bfloat16)
    column_ids = jnp.arange(total, dtype=jnp.int32)

    def block_work(operands):
        teach_blk, stud_blk, pair_blk = operands
        tlog = teacher_scale * inner_rows(teach_blk, capt_b)
        slog = student_scale * inner_rows(stud_blk, capt_b)
        texp = jnp.exp(tlog)
        sexp = jnp.exp(slog)
        zt_sum = lax.optimization_barrier(jnp.sum(texp, axis=1))
        zs_sum = lax.optimization_barrier(jnp.sum(sexp, axis=1))
        acc_sum = lax.optimization_barrier(jnp.sum(texp * (tlog - slog), axis=1))
        hit = column_ids[None, :] == pair_blk[:, None]
        spair = lax.optimization_barrier(jnp.sum(jnp.where(hit, slog, 0.0), axis=1))
        loss_blk = jnp.sum(acc_sum / zt_sum - jnp.log(zt_sum) + 2.0 * jnp.log(zs_sum) - spair)
        coef = (2.0 * sexp / zs_sum[:, None] - texp / zt_sum[:, None] - hit.astype(jnp.float32)).astype(jnp.bfloat16)
        dstud = jnp.dot(coef, capt_b, preferred_element_type=jnp.float32)
        return (loss_blk, dstud)
    block_rows = ROWS_DEV
    loss_parts, dstud = lax.map(block_work, (teach_b.reshape(-1, block_rows, EMBED), stud_b.reshape(-1, block_rows, EMBED), pairing.reshape(-1, block_rows)))
    loss = jnp.sum(loss_parts) / total
    dstud = dstud.reshape(total, EMBED) * (student_scale / total)
    draw = ((dstud - student * lax.optimization_barrier(jnp.sum(student * dstud, axis=1, keepdims=True))) / norm).astype(jnp.bfloat16)
    grad_second = jnp.dot(hidden.T, draw, preferred_element_type=jnp.float32)
    dhid = jnp.dot(draw, w_second.T, preferred_element_type=jnp.float32)
    dpre = gelu_back(dhid)[0].astype(jnp.bfloat16)
    grad_first = jnp.dot(clip_feats.T, dpre, preferred_element_type=jnp.float32)
    return (loss, grad_first, grad_second)
```

```python
import jax
import jax.numpy as jnp
from jax import lax
from jax.sharding import PartitionSpec as P

teacher_scale = 14.0
student_scale = 64.0
eps = 1e-06
gather_bytes = 1 << 23


def normalize(values):
    return values / jnp.sqrt(jnp.sum(values * values, axis=1, keepdims=True) + eps)


def inner_rows(left, right):
    return lax.dot_general(
        left, right, (((1,), (1,)), ((), ())), preferred_element_type=jnp.float32
    )


def inner_cols(left, right):
    return lax.dot_general(
        left, right, (((0,), (0,)), ((), ())), preferred_element_type=jnp.float32
    )


def bits_down(count):
    return [1 << b for b in reversed(range(count.bit_length() - 1))]


def swap(values, axis, bit):
    count = lax.axis_size(axis)
    return lax.ppermute(values, axis, [(i, i ^ bit) for i in range(count)])


def spread(values, axis, bits):
    for bit in bits:
        values = jnp.concatenate([values, swap(values, axis, bit)], axis=0)
    return values


def gelu_exact(values):
    return jax.nn.gelu(values, approximate=False)


def body(clip_feats, teacher_audio, teacher_text, w_first, w_second, pairing):
    rows = clip_feats.shape[0]
    wide_size = lax.axis_size("wide")
    mp_size = lax.axis_size("mp")
    total = rows * wide_size
    part = teacher_text.shape[0]
    half = rows // 2
    wide_bits = bits_down(wide_size)
    mp_bits = bits_down(mp_size)
    wide_index = lax.axis_index("wide")
    mp_index = lax.axis_index("mp")
    side = mp_index % 2
    own_start = side * half

    capt = normalize(teacher_text.astype(jnp.float32)).astype(jnp.bfloat16)
    capt_wide = spread(capt, "wide", wide_bits)
    capt_all = spread(capt_wide, "mp", mp_bits)

    pre_act = jnp.dot(clip_feats, w_first, preferred_element_type=jnp.float32)
    hidden = gelu_exact(pre_act).astype(jnp.bfloat16)
    raw = jnp.dot(hidden, w_second, preferred_element_type=jnp.float32)
    own = lax.dynamic_slice_in_dim(raw, own_start, half, 0)
    other = lax.dynamic_slice_in_dim(raw, half - own_start, half, 0)
    raw = own + swap(other, "mp", 1)
    for bit in reversed(mp_bits[:-1]):
        raw = raw + swap(raw, "mp", bit)
    norm = jnp.sqrt(jnp.sum(raw * raw, axis=1, keepdims=True) + eps)
    student = raw / norm
    stud_b = student.astype(jnp.bfloat16)
    teach = lax.dynamic_slice_in_dim(teacher_audio, own_start, half, 0)
    teach_b = normalize(teach.astype(jnp.float32)).astype(jnp.bfloat16)

    pair = lax.dynamic_slice_in_dim(pairing, own_start, half, 0)
    pair_wide = (pair // (part * mp_size)) ^ wide_index
    pair_mp = (pair // part % mp_size) ^ mp_index
    place = pair % part
    step = part
    for source, bits in ((pair_wide, wide_bits), (pair_mp, mp_bits)):
        for bit in bits:
            place = place + step * ((source // bit) % 2)
            step = step * 2

    scores = inner_rows(jnp.concatenate([teach_b, stud_b], axis=0), capt_all)
    tlog = teacher_scale * scores[:half]
    slog = student_scale * scores[half:]
    hit = jnp.arange(total, dtype=jnp.int32)[None, :] == place[:, None]
    texp = jnp.exp(tlog)
    sexp = jnp.exp(slog)
    zt_sum = jnp.sum(texp, axis=1)
    zs_sum = jnp.sum(sexp, axis=1)
    acc_sum = jnp.sum(texp * (tlog - slog), axis=1)
    spair = jnp.sum(jnp.where(hit, slog, 0.0), axis=1)
    loss = jnp.sum(acc_sum / zt_sum - jnp.log(zt_sum) + 2.0 * jnp.log(zs_sum) - spair)
    coef = (
        2.0 * sexp / zs_sum[:, None] - texp / zt_sum[:, None] - hit.astype(jnp.float32)
    ).astype(jnp.bfloat16)
    dstud = jnp.dot(coef, capt_all, preferred_element_type=jnp.float32) * (student_scale / total)
    draw = ((dstud - student * jnp.sum(student * dstud, axis=1, keepdims=True)) / norm).astype(
        jnp.bfloat16
    )

    if total * clip_feats.shape[1] * 2 <= gather_bytes:
        feats = lax.dynamic_slice_in_dim(clip_feats, own_start, half, 0)
        feats, capt_wide = lax.optimization_barrier((feats, capt_wide))
        feats = spread(spread(feats, "wide", wide_bits), "mp", [1])
        loss_tile = jnp.full((8, 128), loss, jnp.float32)
        for axis, bits in (("wide", wide_bits), ("mp", [1])):
            for bit in bits:
                draw = spread(draw, axis, [bit])
                loss_tile = loss_tile + swap(loss_tile, axis, bit)
        loss = loss_tile[0, 0]
        finish = lambda values: values
    else:
        feats = jnp.concatenate([own_half(clip_feats, own_start, half), own_half(clip_feats, half - own_start, half)])
        draw = spread(draw, "mp", [1])
        finish = lambda values: lax.psum(values, "wide")
        loss = loss + swap(jnp.full((8, 128), loss, jnp.float32), "mp", 1)[0, 0]
    pre_act, gelu_back = jax.vjp(gelu_exact, jnp.dot(feats, w_first, preferred_element_type=jnp.float32))
    hidden = pre_act.astype(jnp.bfloat16)
    grad_second = inner_cols(hidden, draw)
    dpre = gelu_back(inner_rows(draw, w_second))[0].astype(jnp.bfloat16)
    grad_first = inner_cols(feats, dpre)
    grad_first, grad_second, loss = finish((grad_first, grad_second, loss))
    return (loss / total, grad_first, grad_second)


def own_half(values, start, half):
    return lax.dynamic_slice_in_dim(values, start, half, 0)


def solution(mesh):
    return jax.shard_map(
        body,
        mesh=mesh,
        in_specs=(
            P("wide", None),
            P("wide", None),
            P(("wide", "mp"), None),
            P(None, "mp"),
            P("mp", None),
            P("wide"),
        ),
        out_specs=(P(), P(None, "mp"), P("mp", None)),
        check_vma=False,
    )
```

```python
import jax
import jax.numpy as jnp
from jax import lax
from jax.experimental import pallas as pl
from jax.experimental.pallas import tpu as pltpu
from jax.sharding import PartitionSpec as P

teacher_scale = 14.0
student_scale = 64.0
eps = 1e-06
lanes = 128
gather_bytes = 1 << 23


def unit_rows(values):
    values = values.astype(jnp.float32)
    norm = jnp.sqrt(jnp.sum(values * values, axis=1, keepdims=True) + eps)
    return (values / norm).astype(jnp.bfloat16)


def inner_rows(left, right):
    return lax.dot_general(
        left, right, (((1,), (1,)), ((), ())), preferred_element_type=jnp.float32
    )


def inner_cols(left, right):
    return lax.dot_general(
        left, right, (((0,), (0,)), ((), ())), preferred_element_type=jnp.float32
    )


def bits_down(count):
    return [1 << b for b in reversed(range(count.bit_length() - 1))]


def swap(values, axis, bit):
    count = lax.axis_size(axis)
    return lax.ppermute(values, axis, [(i, i ^ bit) for i in range(count)])


def spread(values, steps):
    pieces = [values]
    for axis, bit in steps:
        if len(pieces) > 1:
            values = jnp.concatenate(pieces, axis=0)
            pieces = [values]
        pieces.append(swap(values, axis, bit))
    return pieces


def own_half(values, start, half):
    return lax.dynamic_slice_in_dim(values, start, half, 0)


def in_vmem(count):
    return [pl.BlockSpec(memory_space=pltpu.VMEM)] * count


def loss_step(raw, teach_b, capt_all, place, total):
    rows, width = raw.shape

    def kernel(raw_ref, teach_ref, capt_ref, place_ref, out_ref):
        raw = raw_ref[...]
        norm = jnp.sqrt(jnp.sum(raw * raw, axis=1, keepdims=True) + eps)
        student = raw / norm
        stacked = jnp.concatenate([teach_ref[...], student.astype(jnp.bfloat16)], axis=0)
        scores = inner_rows(stacked, capt_ref[...])
        tlog = teacher_scale * scores[:rows]
        slog = student_scale * scores[rows:]
        texp = jnp.exp(tlog)
        sexp = jnp.exp(slog)
        hit = lax.broadcasted_iota(jnp.int32, tlog.shape, 1) == place_ref[...]
        zt_sum = jnp.sum(texp, axis=1, keepdims=True)
        zs_sum = jnp.sum(sexp, axis=1, keepdims=True)
        acc_sum = jnp.sum(texp * (tlog - slog), axis=1, keepdims=True)
        spair = jnp.sum(jnp.where(hit, slog, 0.0), axis=1, keepdims=True)
        coef = 2.0 / zs_sum * sexp - 1.0 / zt_sum * texp - jnp.where(hit, 1.0, 0.0)
        dstud = jnp.dot(
            coef.astype(jnp.bfloat16), capt_ref[...], preferred_element_type=jnp.float32
        ) * (student_scale / total)
        along = jnp.sum(student * dstud, axis=1, keepdims=True)
        draw = ((dstud - student * along) / norm).astype(jnp.bfloat16)
        for index in range(width // lanes):
            out_ref[index * rows : (index + 1) * rows, :] = draw[
                :, index * lanes : (index + 1) * lanes
            ]
        loss = acc_sum / zt_sum - jnp.log(zt_sum) + 2.0 * jnp.log(zs_sum) - spair
        rest = jnp.broadcast_to(jnp.sum(loss, axis=0, keepdims=True), (8, lanes))
        row = lax.broadcasted_iota(jnp.int32, rest.shape, 0)
        lane = lax.broadcasted_iota(jnp.int32, rest.shape, 1)
        packed = jnp.zeros_like(rest)
        for index in range(3):
            term = rest.astype(jnp.bfloat16).astype(jnp.float32)
            packed = jnp.where((row == 0) & (lane == index), term, packed)
            rest = rest - term
        out_ref[width // lanes * rows :, :] = packed.astype(jnp.bfloat16)

    return pl.pallas_call(
        kernel,
        out_shape=jax.ShapeDtypeStruct((rows * width // lanes + 8, lanes), jnp.bfloat16),
        in_specs=in_vmem(4),
        out_specs=in_vmem(1)[0],
        compiler_params=pltpu.CompilerParams(vmem_limit_bytes=16 << 20),
        name="loss_step",
    )(raw, teach_b, capt_all, place)


def unpacked(ref, rows, width):
    step = rows * width // lanes + 8
    draws, tiles = [], []
    for base in range(0, ref.shape[0], step):
        draws.append(
            jnp.concatenate(
                [ref[base + k * rows : base + (k + 1) * rows, :] for k in range(width // lanes)],
                axis=1,
            )
        )
        tiles.append(ref[base + step - 8 : base + step, :].astype(jnp.float32))
    return jnp.concatenate(draws, axis=0), sum(tiles)


def first_grads(packed, starts, last_starts, feats, hidden_t, slope_t, weight, rows):
    units, width, depth = hidden_t.shape[0], weight.shape[1], feats[0].shape[1]
    step = rows * width // lanes + 8
    bounds = [0]
    for values in feats:
        bounds.append(bounds[-1] + values.shape[0])
    stops = [start + values.shape[0] // step * rows for start, values in zip(starts, packed)]
    last_stops = [start + rest for start, rest in zip(last_starts, [bounds[-1] // 2 - stops[0]] * 2)]

    def kernel(*refs):
        packed_refs, feat_refs = refs[: len(packed)], refs[len(packed) : len(packed) + len(feats)]
        hidden_ref, slope_ref, weight_ref, first_ref, second_ref, tile_ref, last_ref = refs[-7:]

        def feat_rows(start, stop):
            return jnp.concatenate(
                [
                    ref[max(low, start) - low : min(high, stop) - low, :]
                    for ref, low, high in zip(feat_refs, bounds, bounds[1:])
                    if max(low, start) < min(high, stop)
                ],
                axis=0,
            )

        first, second, tile = [], [], []
        for ref, start, stop in zip(packed_refs, starts, stops):
            draw, part = unpacked(ref, rows, width)
            dpre = (inner_rows(weight_ref[...], draw) * slope_ref[:, start:stop]).astype(
                jnp.bfloat16
            )
            second.append(
                jnp.dot(hidden_ref[:, start:stop], draw, preferred_element_type=jnp.float32)
            )
            first.append(
                jnp.dot(dpre, feat_rows(start, stop), preferred_element_type=jnp.float32)
            )
            tile.append(part)
        first_ref[...] = sum(first).T
        second_ref[...] = sum(second)
        tile_ref[...] = sum(tile)
        last = [feat_rows(start, stop) for start, stop in zip(last_starts, last_stops)]
        last_ref[...] = jnp.concatenate(last, axis=0).T

    count = sum(stop - start for start, stop in zip(last_starts, last_stops))
    return pl.pallas_call(
        kernel,
        out_shape=(
            jax.ShapeDtypeStruct((depth, units), jnp.float32),
            jax.ShapeDtypeStruct((units, width), jnp.float32),
            jax.ShapeDtypeStruct((8, lanes), jnp.float32),
            jax.ShapeDtypeStruct((depth, count), jnp.bfloat16),
        ),
        in_specs=in_vmem(len(packed) + len(feats) + 3),
        out_specs=in_vmem(4),
        compiler_params=pltpu.CompilerParams(vmem_limit_bytes=16 << 20),
        name="first_grads",
    )(*packed, *feats, hidden_t, slope_t, weight)


def last_grads(packed, starts, sums, hidden_t, slope_t, weight, rows, total):
    units, width, depth = hidden_t.shape[0], weight.shape[1], sums[0].shape[0]

    def kernel(*refs):
        packed_refs = refs[: len(packed)]
        hidden_ref, slope_ref, weight_ref, first_ref, second_ref, tile_ref, feats_ref = refs[
            len(packed) : -3
        ]
        loss_out, first_out, second_out = refs[-3:]
        draws, tiles = zip(*(unpacked(ref, rows, width) for ref in packed_refs))
        draw = jnp.concatenate(draws, axis=0)
        columns = [
            slice(start, start + values.shape[0]) for start, values in zip(starts, draws)
        ]
        slope = jnp.concatenate([slope_ref[:, part] for part in columns], axis=1)
        hidden = jnp.concatenate([hidden_ref[:, part] for part in columns], axis=1)
        dpre = (inner_rows(weight_ref[...], draw) * slope).astype(jnp.bfloat16)
        first_out[...] = first_ref[...] + inner_rows(feats_ref[...], dpre)
        second_out[...] = second_ref[...] + jnp.dot(
            hidden, draw, preferred_element_type=jnp.float32
        )
        loss_out[0, 0] = jnp.sum(tile_ref[...] + sum(tiles)) / total

    return pl.pallas_call(
        kernel,
        out_shape=(
            jax.ShapeDtypeStruct((1, 1), jnp.float32),
            jax.ShapeDtypeStruct((depth, units), jnp.float32),
            jax.ShapeDtypeStruct((units, width), jnp.float32),
        ),
        in_specs=in_vmem(len(packed) + 7),
        out_specs=[pl.BlockSpec(memory_space=pltpu.SMEM)] + in_vmem(2),
        compiler_params=pltpu.CompilerParams(vmem_limit_bytes=16 << 20),
        name="last_grads",
    )(*packed, hidden_t, slope_t, weight, *sums)


def stage(values):
    def kernel(values_ref, copy_ref):
        copy_ref[...] = values_ref[...]

    return pl.pallas_call(
        kernel,
        out_shape=jax.ShapeDtypeStruct(values.shape, values.dtype),
        in_specs=[pl.BlockSpec(memory_space=pltpu.VMEM)],
        out_specs=pl.BlockSpec(memory_space=pltpu.VMEM),
        compiler_params=pltpu.CompilerParams(vmem_limit_bytes=1 << 20),
        name="stage",
    )(values)


def gelu_exact(values):
    return jax.nn.gelu(values, approximate=False)


def body(clip_feats, teacher_audio, teacher_text, w_first, w_second, pairing):
    rows = clip_feats.shape[0]
    wide_size = lax.axis_size("wide")
    mp_size = lax.axis_size("mp")
    total = rows * wide_size
    part = teacher_text.shape[0]
    half = rows // 2
    wide_bits = bits_down(wide_size)
    mp_bits = bits_down(mp_size)
    own_start = lax.axis_index("mp") % 2 * half

    far_bits, near_bit = wide_bits[:-1], wide_bits[-1]
    far_steps = [("wide", bit) for bit in far_bits]
    gathers = gathers_rows(total, clip_feats.shape[1])

    block = jnp.concatenate(spread(teacher_text, far_steps), axis=0)
    across = swap(block, "wide", near_bit)
    beside = swap(block, "mp", mp_bits[0])
    corner = swap(across, "mp", mp_bits[0])
    most = jnp.concatenate([unit_rows(block), unit_rows(beside), unit_rows(across)], axis=0)
    corner = unit_rows(corner)
    capt_all = jnp.concatenate([most, corner, swap(most, "mp", 1), swap(corner, "mp", 1)], axis=0)
    places = [("wide", bit) for bit in far_bits]
    places += [("mp", mp_bits[0]), ("wide", near_bit), ("mp", 1)]

    pre_act = jnp.dot(clip_feats, w_first, preferred_element_type=jnp.float32)
    hidden = gelu_exact(pre_act).astype(jnp.bfloat16)
    raw = jnp.dot(hidden, w_second, preferred_element_type=jnp.float32)
    own = own_half(raw, own_start, half)
    raw = own + swap(own_half(raw, half - own_start, half), "mp", 1)
    raw = raw + swap(raw, "mp", mp_bits[0])
    teach_b = unit_rows(own_half(teacher_audio, own_start, half))

    place = places_of(own_half(pairing, own_start, half), part, places)

    if not gathers:
        return summed_grads(
            clip_feats, own_start, hidden, pre_act, raw, teach_b, capt_all, place, w_second, total
        )

    draw = loss_step(raw, teach_b, capt_all, place, total)
    feats = spread(own_half(clip_feats, own_start, half), far_steps)
    feats = [
        jnp.concatenate(feats, axis=0),
        swap(jnp.concatenate(feats[:-1], axis=0), "wide", near_bit),
        swap(feats[-1], "wide", near_bit),
    ]
    feats.append(swap(jnp.concatenate(feats, axis=0), "mp", 1))
    draws = spread(draw, far_steps)
    across = swap(jnp.concatenate(draws[:-1], axis=0), "wide", near_bit)
    last = swap(draws[-1], "wide", near_bit)
    most = jnp.concatenate([*draws, across], axis=0)
    most = [most, swap(most, "mp", 1)]
    last = [last, swap(last, "mp", 1)]
    pre_t = jnp.concatenate(
        [
            lax.dot_general(
                w_first, rows, (((0,), (1,)), ((), ())), preferred_element_type=jnp.float32
            )
            for rows in feats
        ],
        axis=1,
    )
    gelu_t, gelu_back = jax.vjp(gelu_exact, pre_t)
    slope_t = gelu_back(jnp.ones_like(pre_t))[0]
    hidden_t = gelu_t.astype(jnp.bfloat16)
    factors = (hidden_t, slope_t, stage(w_second))
    rest = rows_of(last[0], draw, half)
    starts = [0, total // 2]
    last_starts = [total // 2 - rest, total - rest]
    sums = first_grads(most, starts, last_starts, feats, *factors, half)
    loss, grad_first, grad_second = last_grads(last, last_starts, sums, *factors, half, total)
    return (loss[0, 0], grad_first, grad_second)


def rows_of(packed, block, half):
    return packed.shape[0] // block.shape[0] * half


def places_of(pair, part, places):
    mp_size = lax.axis_size("mp")
    differs = {
        "wide": (pair // (part * mp_size)) ^ lax.axis_index("wide"),
        "mp": (pair // part % mp_size) ^ lax.axis_index("mp"),
    }
    place = pair % part
    for index, (axis, bit) in enumerate(places):
        place = place + (part << index) * (differs[axis] // bit % 2)
    return place[:, None]


def summed_grads(
    clip_feats, own_start, hidden, pre_act, raw, teach_b, capt_all, place, w_second, total
):
    half = raw.shape[0]
    gelu_back = jax.vjp(gelu_exact, pre_act)[1]
    norm = jnp.sqrt(jnp.sum(raw * raw, axis=1, keepdims=True) + eps)
    student = raw / norm
    stud_b = student.astype(jnp.bfloat16)
    scores = inner_rows(jnp.concatenate([teach_b, stud_b], axis=0), capt_all)
    tlog = teacher_scale * scores[:half]
    slog = student_scale * scores[half:]
    hit = jnp.arange(total, dtype=jnp.int32)[None, :] == place
    texp = jnp.exp(tlog)
    sexp = jnp.exp(slog)
    zt_sum = jnp.sum(texp, axis=1)
    zs_sum = jnp.sum(sexp, axis=1)
    acc_sum = jnp.sum(texp * (tlog - slog), axis=1)
    spair = jnp.sum(jnp.where(hit, slog, 0.0), axis=1)
    loss = jnp.sum(acc_sum / zt_sum - jnp.log(zt_sum) + 2.0 * jnp.log(zs_sum) - spair)
    coef = (
        2.0 * sexp / zs_sum[:, None] - texp / zt_sum[:, None] - hit.astype(jnp.float32)
    ).astype(jnp.bfloat16)
    dstud = jnp.dot(coef, capt_all, preferred_element_type=jnp.float32) * (student_scale / total)
    draw = ((dstud - student * jnp.sum(student * dstud, axis=1, keepdims=True)) / norm).astype(
        jnp.bfloat16
    )

    draw = jnp.concatenate([draw, swap(draw, "mp", 1)], axis=0)
    draw = jnp.where(own_start > 0, jnp.roll(draw, half, axis=0), draw)
    grad_second = inner_cols(hidden, draw)
    dpre = gelu_back(inner_rows(draw, w_second))[0].astype(jnp.bfloat16)
    grad_first = inner_cols(clip_feats, dpre)
    tile = jnp.full((8, 128), loss, jnp.float32)
    loss = (tile + swap(tile, "mp", 1))[0, 0]
    grad_first, grad_second, loss = lax.psum((grad_first, grad_second, loss), "wide")
    return (loss / total, grad_first, grad_second)


def gathers_rows(total, depth):
    return 2 * total * depth <= gather_bytes


def solution(mesh):
    return jax.shard_map(
        body,
        mesh=mesh,
        in_specs=(
            P("wide", None),
            P("wide", None),
            P(("wide", "mp"), None),
            P(None, "mp"),
            P("mp", None),
            P("wide"),
        ),
        out_specs=(P(), P(None, "mp"), P("mp", None)),
        check_vma=False,
    )
```

```python
import jax
import jax.numpy as jnp
from jax import lax
from jax.experimental import pallas as pl
from jax.experimental.pallas import tpu as pltpu
from jax.sharding import PartitionSpec as P

teacher_scale = 14.0
student_scale = 64.0
eps = 1e-06
lanes = 128
gather_bytes = 1 << 23


def unit_rows(values):
    values = values.astype(jnp.float32)
    norm = jnp.sqrt(jnp.sum(values * values, axis=1, keepdims=True) + eps)
    return (values / norm).astype(jnp.bfloat16)


def inner_rows(left, right):
    return lax.dot_general(
        left, right, (((1,), (1,)), ((), ())), preferred_element_type=jnp.float32
    )


def inner_cols(left, right):
    return lax.dot_general(
        left, right, (((0,), (0,)), ((), ())), preferred_element_type=jnp.float32
    )


def bits_down(count):
    return [1 << b for b in reversed(range(count.bit_length() - 1))]


def swap(values, axis, bit):
    count = lax.axis_size(axis)
    return lax.ppermute(values, axis, [(i, i ^ bit) for i in range(count)])


def spread(values, steps):
    pieces = [values]
    for axis, bit in steps:
        if len(pieces) > 1:
            values = jnp.concatenate(pieces, axis=0)
            pieces = [values]
        pieces.append(swap(values, axis, bit))
    return pieces


def own_half(values, start, half):
    return lax.dynamic_slice_in_dim(values, start, half, 0)


def in_vmem(count):
    return [pl.BlockSpec(memory_space=pltpu.VMEM)] * count


def loss_step(raw, teach_b, capt_all, place, total):
    rows, width = raw.shape

    def kernel(raw_ref, teach_ref, capt_ref, place_ref, out_ref):
        raw = raw_ref[...]
        norm = jnp.sqrt(jnp.sum(raw * raw, axis=1, keepdims=True) + eps)
        student = raw / norm
        stacked = jnp.concatenate([teach_ref[...], student.astype(jnp.bfloat16)], axis=0)
        scores = inner_rows(stacked, capt_ref[...])
        tlog = teacher_scale * scores[:rows]
        slog = student_scale * scores[rows:]
        texp = jnp.exp(tlog)
        sexp = jnp.exp(slog)
        hit = lax.broadcasted_iota(jnp.int32, tlog.shape, 1) == place_ref[...]
        zt_sum = jnp.sum(texp, axis=1, keepdims=True)
        zs_sum = jnp.sum(sexp, axis=1, keepdims=True)
        acc_sum = jnp.sum(texp * (tlog - slog), axis=1, keepdims=True)
        spair = jnp.sum(jnp.where(hit, slog, 0.0), axis=1, keepdims=True)
        coef = 2.0 / zs_sum * sexp - 1.0 / zt_sum * texp - jnp.where(hit, 1.0, 0.0)
        dstud = jnp.dot(
            coef.astype(jnp.bfloat16), capt_ref[...], preferred_element_type=jnp.float32
        ) * (student_scale / total)
        along = jnp.sum(student * dstud, axis=1, keepdims=True)
        draw = ((dstud - student * along) / norm).astype(jnp.bfloat16)
        for index in range(width // lanes):
            out_ref[index * rows : (index + 1) * rows, :] = draw[
                :, index * lanes : (index + 1) * lanes
            ]
        loss = acc_sum / zt_sum - jnp.log(zt_sum) + 2.0 * jnp.log(zs_sum) - spair
        rest = jnp.broadcast_to(jnp.sum(loss, axis=0, keepdims=True), (8, lanes))
        row = lax.broadcasted_iota(jnp.int32, rest.shape, 0)
        lane = lax.broadcasted_iota(jnp.int32, rest.shape, 1)
        packed = jnp.zeros_like(rest)
        for index in range(3):
            term = rest.astype(jnp.bfloat16).astype(jnp.float32)
            packed = jnp.where((row == 0) & (lane == index), term, packed)
            rest = rest - term
        out_ref[width // lanes * rows :, :] = packed.astype(jnp.bfloat16)

    return pl.pallas_call(
        kernel,
        out_shape=jax.ShapeDtypeStruct((rows * width // lanes + 8, lanes), jnp.bfloat16),
        in_specs=in_vmem(4),
        out_specs=in_vmem(1)[0],
        compiler_params=pltpu.CompilerParams(vmem_limit_bytes=16 << 20),
        name="loss_step",
    )(raw, teach_b, capt_all, place)


def unpacked(ref, rows, width):
    step = rows * width // lanes + 8
    draws, tiles = [], []
    for base in range(0, ref.shape[0], step):
        draws.append(
            jnp.concatenate(
                [ref[base + k * rows : base + (k + 1) * rows, :] for k in range(width // lanes)],
                axis=1,
            )
        )
        tiles.append(ref[base + step - 8 : base + step, :].astype(jnp.float32))
    return jnp.concatenate(draws, axis=0), sum(tiles)


def first_grads(packed, starts, last_starts, feats, hidden_t, slope_t, weight, rows):
    units, width, depth = hidden_t.shape[0], weight.shape[1], feats[0].shape[1]
    step = rows * width // lanes + 8
    bounds = [0]
    for values in feats:
        bounds.append(bounds[-1] + values.shape[0])
    stops = [start + values.shape[0] // step * rows for start, values in zip(starts, packed)]
    last_stops = [start + rest for start, rest in zip(last_starts, [bounds[-1] // 2 - stops[0]] * 2)]

    def kernel(*refs):
        packed_refs, feat_refs = refs[: len(packed)], refs[len(packed) : len(packed) + len(feats)]
        hidden_ref, slope_ref, weight_ref, first_ref, second_ref, tile_ref, last_ref = refs[-7:]

        def feat_rows(start, stop):
            return jnp.concatenate(
                [
                    ref[max(low, start) - low : min(high, stop) - low, :]
                    for ref, low, high in zip(feat_refs, bounds, bounds[1:])
                    if max(low, start) < min(high, stop)
                ],
                axis=0,
            )

        first, second, tile = [], [], []
        for ref, start, stop in zip(packed_refs, starts, stops):
            draw, part = unpacked(ref, rows, width)
            dpre = (inner_rows(weight_ref[...], draw) * slope_ref[:, start:stop]).astype(
                jnp.bfloat16
            )
            second.append(
                jnp.dot(hidden_ref[:, start:stop], draw, preferred_element_type=jnp.float32)
            )
            first.append(
                jnp.dot(dpre, feat_rows(start, stop), preferred_element_type=jnp.float32)
            )
            tile.append(part)
        first_ref[...] = sum(first).T
        second_ref[...] = sum(second)
        tile_ref[...] = sum(tile)
        last = [feat_rows(start, stop) for start, stop in zip(last_starts, last_stops)]
        last_ref[...] = jnp.concatenate(last, axis=0).T

    count = sum(stop - start for start, stop in zip(last_starts, last_stops))
    return pl.pallas_call(
        kernel,
        out_shape=(
            jax.ShapeDtypeStruct((depth, units), jnp.float32),
            jax.ShapeDtypeStruct((units, width), jnp.float32),
            jax.ShapeDtypeStruct((8, lanes), jnp.float32),
            jax.ShapeDtypeStruct((depth, count), jnp.bfloat16),
        ),
        in_specs=in_vmem(len(packed) + len(feats) + 3),
        out_specs=in_vmem(4),
        compiler_params=pltpu.CompilerParams(vmem_limit_bytes=16 << 20),
        name="first_grads",
    )(*packed, *feats, hidden_t, slope_t, weight)


def last_grads(packed, starts, sums, hidden_t, slope_t, weight, rows, total):
    units, width, depth = hidden_t.shape[0], weight.shape[1], sums[0].shape[0]

    def kernel(*refs):
        packed_refs = refs[: len(packed)]
        hidden_ref, slope_ref, weight_ref, first_ref, second_ref, tile_ref, feats_ref = refs[
            len(packed) : -3
        ]
        loss_out, first_out, second_out = refs[-3:]
        draws, tiles = zip(*(unpacked(ref, rows, width) for ref in packed_refs))
        draw = jnp.concatenate(draws, axis=0)
        columns = [
            slice(start, start + values.shape[0]) for start, values in zip(starts, draws)
        ]
        slope = jnp.concatenate([slope_ref[:, part] for part in columns], axis=1)
        hidden = jnp.concatenate([hidden_ref[:, part] for part in columns], axis=1)
        dpre = (inner_rows(weight_ref[...], draw) * slope).astype(jnp.bfloat16)
        first_out[...] = first_ref[...] + inner_rows(feats_ref[...], dpre)
        second_out[...] = second_ref[...] + jnp.dot(
            hidden, draw, preferred_element_type=jnp.float32
        )
        loss_out[0, 0] = jnp.sum(tile_ref[...] + sum(tiles)) / total

    return pl.pallas_call(
        kernel,
        out_shape=(
            jax.ShapeDtypeStruct((1, 1), jnp.float32),
            jax.ShapeDtypeStruct((depth, units), jnp.float32),
            jax.ShapeDtypeStruct((units, width), jnp.float32),
        ),
        in_specs=in_vmem(len(packed) + 7),
        out_specs=[pl.BlockSpec(memory_space=pltpu.SMEM)] + in_vmem(2),
        compiler_params=pltpu.CompilerParams(vmem_limit_bytes=16 << 20),
        name="last_grads",
    )(*packed, hidden_t, slope_t, weight, *sums)


def stage(values):
    def kernel(values_ref, copy_ref):
        copy_ref[...] = values_ref[...]

    return pl.pallas_call(
        kernel,
        out_shape=jax.ShapeDtypeStruct(values.shape, values.dtype),
        in_specs=[pl.BlockSpec(memory_space=pltpu.VMEM)],
        out_specs=pl.BlockSpec(memory_space=pltpu.VMEM),
        compiler_params=pltpu.CompilerParams(vmem_limit_bytes=1 << 20),
        name="stage",
    )(values)


def gelu_exact(values):
    return jax.nn.gelu(values, approximate=False)


def body(clip_feats, teacher_audio, teacher_text, w_first, w_second, pairing):
    rows = clip_feats.shape[0]
    wide_size = lax.axis_size("wide")
    mp_size = lax.axis_size("mp")
    total = rows * wide_size
    part = teacher_text.shape[0]
    half = rows // 2
    wide_bits = bits_down(wide_size)
    mp_bits = bits_down(mp_size)
    own_start = lax.axis_index("mp") % 2 * half

    far_bits, near_bit = wide_bits[:-1], wide_bits[-1]
    far_steps = [("wide", bit) for bit in far_bits]
    gathers = len(far_bits) > 1 and gathers_rows(total, clip_feats.shape[1])

    block = jnp.concatenate(spread(teacher_text, far_steps), axis=0)
    across = swap(block, "wide", near_bit)
    beside = swap(block, "mp", mp_bits[0])
    corner = swap(across, "mp", mp_bits[0])
    most = jnp.concatenate([unit_rows(block), unit_rows(beside), unit_rows(across)], axis=0)
    corner = unit_rows(corner)
    capt_all = jnp.concatenate([most, corner, swap(most, "mp", 1), swap(corner, "mp", 1)], axis=0)
    places = [("wide", bit) for bit in far_bits]
    places += [("mp", mp_bits[0]), ("wide", near_bit), ("mp", 1)]

    pre_act = jnp.dot(clip_feats, w_first, preferred_element_type=jnp.float32)
    hidden = gelu_exact(pre_act).astype(jnp.bfloat16)
    raw = jnp.dot(hidden, w_second, preferred_element_type=jnp.float32)
    own = own_half(raw, own_start, half)
    raw = own + swap(own_half(raw, half - own_start, half), "mp", 1)
    raw = raw + swap(raw, "mp", mp_bits[0])
    teach_b = unit_rows(own_half(teacher_audio, own_start, half))

    place = places_of(own_half(pairing, own_start, half), part, places)

    if not gathers:
        return summed_grads(
            clip_feats, own_start, hidden, pre_act, raw, teach_b, capt_all, place, w_second, total
        )

    draw = loss_step(raw, teach_b, capt_all, place, total)
    draws = [draw]
    for index, bit in enumerate(far_bits):
        prior = jnp.concatenate(draws, axis=0)
        fresh = swap(prior, "wide", bit)
        draws = [prior, fresh]
        if not index:
            first_step = fresh
    across = swap(prior, "wide", near_bit)
    last = swap(fresh, "wide", near_bit)
    most = jnp.concatenate([prior, fresh, across], axis=0)
    most = [most, swap(most, "mp", 1)]
    rest = rows_of(last, draw, half)
    last = [last, swap(last, "mp", 1)]

    near = own_half(clip_feats, own_start, half)
    near, moved = spread(near, [("wide", bit) for bit in reversed(far_bits)])
    pairs = [
        (near, moved),
        (swap(near, "wide", near_bit), swap(moved, "wide", near_bit)),
    ]
    pairs, _ = lax.optimization_barrier((pairs, first_step))
    masks, turned = [0], [0]
    for bit in far_bits:
        masks += [mask ^ bit for mask in masks]
    for bit in reversed(far_bits):
        turned += [mask ^ bit for mask in turned]
    feats = []
    for pair in pairs:
        blocks = [block for values in pair for block in jnp.split(values, len(masks) // 2)]
        feats.append(jnp.concatenate([blocks[turned.index(mask)] for mask in masks], axis=0))
    feats.append(swap(jnp.concatenate(feats, axis=0), "mp", 1))

    pre_t = jnp.concatenate(
        [
            lax.dot_general(
                w_first, rows, (((0,), (1,)), ((), ())), preferred_element_type=jnp.float32
            )
            for rows in feats
        ],
        axis=1,
    )
    gelu_t, gelu_back = jax.vjp(gelu_exact, pre_t)
    slope_t = gelu_back(jnp.ones_like(pre_t))[0]
    hidden_t = gelu_t.astype(jnp.bfloat16)
    factors = (hidden_t, slope_t, stage(w_second))
    starts = [0, total // 2]
    last_starts = [total // 2 - rest, total - rest]
    sums = first_grads(most, starts, last_starts, feats, *factors, half)
    loss, grad_first, grad_second = last_grads(last, last_starts, sums, *factors, half, total)
    return (loss[0, 0], grad_first, grad_second)


def rows_of(packed, block, half):
    return packed.shape[0] // block.shape[0] * half


def places_of(pair, part, places):
    mp_size = lax.axis_size("mp")
    differs = {
        "wide": (pair // (part * mp_size)) ^ lax.axis_index("wide"),
        "mp": (pair // part % mp_size) ^ lax.axis_index("mp"),
    }
    place = pair % part
    for index, (axis, bit) in enumerate(places):
        place = place + (part << index) * (differs[axis] // bit % 2)
    return place[:, None]


def summed_grads(
    clip_feats, own_start, hidden, pre_act, raw, teach_b, capt_all, place, w_second, total
):
    half = raw.shape[0]
    gelu_back = jax.vjp(gelu_exact, pre_act)[1]
    norm = jnp.sqrt(jnp.sum(raw * raw, axis=1, keepdims=True) + eps)
    student = raw / norm
    stud_b = student.astype(jnp.bfloat16)
    scores = inner_rows(jnp.concatenate([teach_b, stud_b], axis=0), capt_all)
    tlog = teacher_scale * scores[:half]
    slog = student_scale * scores[half:]
    hit = jnp.arange(total, dtype=jnp.int32)[None, :] == place
    texp = jnp.exp(tlog)
    sexp = jnp.exp(slog)
    zt_sum = jnp.sum(texp, axis=1)
    zs_sum = jnp.sum(sexp, axis=1)
    acc_sum = jnp.sum(texp * (tlog - slog), axis=1)
    spair = jnp.sum(jnp.where(hit, slog, 0.0), axis=1)
    loss = jnp.sum(acc_sum / zt_sum - jnp.log(zt_sum) + 2.0 * jnp.log(zs_sum) - spair)
    coef = (
        2.0 * sexp / zs_sum[:, None] - texp / zt_sum[:, None] - hit.astype(jnp.float32)
    ).astype(jnp.bfloat16)
    dstud = jnp.dot(coef, capt_all, preferred_element_type=jnp.float32) * (student_scale / total)
    draw = ((dstud - student * jnp.sum(student * dstud, axis=1, keepdims=True)) / norm).astype(
        jnp.bfloat16
    )

    draw = jnp.concatenate([draw, swap(draw, "mp", 1)], axis=0)
    draw = jnp.where(own_start > 0, jnp.roll(draw, half, axis=0), draw)
    grad_second = inner_cols(hidden, draw)
    dpre = gelu_back(inner_rows(draw, w_second))[0].astype(jnp.bfloat16)
    grad_first = inner_cols(clip_feats, dpre)
    tile = jnp.full((8, 128), loss, jnp.float32)
    loss = (tile + swap(tile, "mp", 1))[0, 0]
    grad_first, grad_second, loss = lax.psum((grad_first, grad_second, loss), "wide")
    return (loss / total, grad_first, grad_second)


def gathers_rows(total, depth):
    return 2 * total * depth <= gather_bytes


def solution(mesh):
    return jax.shard_map(
        body,
        mesh=mesh,
        in_specs=(
            P("wide", None),
            P("wide", None),
            P(("wide", "mp"), None),
            P(None, "mp"),
            P("mp", None),
            P("wide"),
        ),
        out_specs=(P(), P(None, "mp"), P("mp", None)),
        check_vma=False,
    )
```

```python
import jax
import jax.numpy as jnp
from jax import lax
from jax.experimental import pallas as pl
from jax.experimental.pallas import tpu as pltpu
from jax.sharding import PartitionSpec as P

teacher_scale = 14.0
student_scale = 64.0
eps = 1e-06
lanes = 128
gather_bytes = 1 << 23


def unit_rows(values):
    values = values.astype(jnp.float32)
    norm = jnp.sqrt(jnp.sum(values * values, axis=1, keepdims=True) + eps)
    return (values / norm).astype(jnp.bfloat16)


def inner_rows(left, right):
    return lax.dot_general(
        left, right, (((1,), (1,)), ((), ())), preferred_element_type=jnp.float32
    )


def inner_cols(left, right):
    return lax.dot_general(
        left, right, (((0,), (0,)), ((), ())), preferred_element_type=jnp.float32
    )


def bits_down(count):
    return [1 << b for b in reversed(range(count.bit_length() - 1))]


def swap(values, axis, bit):
    count = lax.axis_size(axis)
    return lax.ppermute(values, axis, [(i, i ^ bit) for i in range(count)])


def spread(values, steps):
    pieces = [values]
    for axis, bit in steps:
        if len(pieces) > 1:
            values = jnp.concatenate(pieces, axis=0)
            pieces = [values]
        pieces.append(swap(values, axis, bit))
    return pieces


def own_half(values, start, half):
    return lax.dynamic_slice_in_dim(values, start, half, 0)


def in_vmem(count):
    return [pl.BlockSpec(memory_space=pltpu.VMEM)] * count


def loss_step(raw, teach_b, capt_all, place, total):
    rows, width = raw.shape

    def kernel(raw_ref, teach_ref, capt_ref, place_ref, out_ref):
        raw = raw_ref[...]
        norm = jnp.sqrt(jnp.sum(raw * raw, axis=1, keepdims=True) + eps)
        student = raw / norm
        stacked = jnp.concatenate([teach_ref[...], student.astype(jnp.bfloat16)], axis=0)
        scores = inner_rows(stacked, capt_ref[...])
        tlog = teacher_scale * scores[:rows]
        slog = student_scale * scores[rows:]
        texp = jnp.exp(tlog)
        sexp = jnp.exp(slog)
        hit = lax.broadcasted_iota(jnp.int32, tlog.shape, 1) == place_ref[...]
        zt_sum = jnp.sum(texp, axis=1, keepdims=True)
        zs_sum = jnp.sum(sexp, axis=1, keepdims=True)
        acc_sum = jnp.sum(texp * (tlog - slog), axis=1, keepdims=True)
        spair = jnp.sum(jnp.where(hit, slog, 0.0), axis=1, keepdims=True)
        coef = 2.0 / zs_sum * sexp - 1.0 / zt_sum * texp - jnp.where(hit, 1.0, 0.0)
        dstud = jnp.dot(
            coef.astype(jnp.bfloat16), capt_ref[...], preferred_element_type=jnp.float32
        ) * (student_scale / total)
        along = jnp.sum(student * dstud, axis=1, keepdims=True)
        draw = ((dstud - student * along) / norm).astype(jnp.bfloat16)
        for index in range(width // lanes):
            out_ref[index * rows : (index + 1) * rows, :] = draw[
                :, index * lanes : (index + 1) * lanes
            ]
        loss = acc_sum / zt_sum - jnp.log(zt_sum) + 2.0 * jnp.log(zs_sum) - spair
        rest = jnp.broadcast_to(jnp.sum(loss, axis=0, keepdims=True), (8, lanes))
        row = lax.broadcasted_iota(jnp.int32, rest.shape, 0)
        lane = lax.broadcasted_iota(jnp.int32, rest.shape, 1)
        packed = jnp.zeros_like(rest)
        for index in range(3):
            term = rest.astype(jnp.bfloat16).astype(jnp.float32)
            packed = jnp.where((row == 0) & (lane == index), term, packed)
            rest = rest - term
        out_ref[width // lanes * rows :, :] = packed.astype(jnp.bfloat16)

    return pl.pallas_call(
        kernel,
        out_shape=jax.ShapeDtypeStruct((rows * width // lanes + 8, lanes), jnp.bfloat16),
        in_specs=in_vmem(4),
        out_specs=in_vmem(1)[0],
        compiler_params=pltpu.CompilerParams(vmem_limit_bytes=16 << 20),
        name="loss_step",
    )(raw, teach_b, capt_all, place)


def unpacked(ref, rows, width):
    step = rows * width // lanes + 8
    draws, tiles = [], []
    for base in range(0, ref.shape[0], step):
        draws.append(
            jnp.concatenate(
                [ref[base + k * rows : base + (k + 1) * rows, :] for k in range(width // lanes)],
                axis=1,
            )
        )
        tiles.append(ref[base + step - 8 : base + step, :].astype(jnp.float32))
    return jnp.concatenate(draws, axis=0), sum(tiles)


def first_grads(packed, starts, last_starts, feats, hidden_t, slope_t, weight, rows):
    units, width, depth = hidden_t.shape[0], weight.shape[1], feats[0].shape[1]
    step = rows * width // lanes + 8
    bounds = [0]
    for values in feats:
        bounds.append(bounds[-1] + values.shape[0])
    stops = [start + values.shape[0] // step * rows for start, values in zip(starts, packed)]
    last_stops = [start + rest for start, rest in zip(last_starts, [bounds[-1] // 2 - stops[0]] * 2)]

    def kernel(*refs):
        packed_refs, feat_refs = refs[: len(packed)], refs[len(packed) : len(packed) + len(feats)]
        hidden_ref, slope_ref, weight_ref, first_ref, second_ref, tile_ref, last_ref = refs[-7:]

        def feat_rows(start, stop):
            return jnp.concatenate(
                [
                    ref[max(low, start) - low : min(high, stop) - low, :]
                    for ref, low, high in zip(feat_refs, bounds, bounds[1:])
                    if max(low, start) < min(high, stop)
                ],
                axis=0,
            )

        first, second, tile = [], [], []
        for ref, start, stop in zip(packed_refs, starts, stops):
            draw, part = unpacked(ref, rows, width)
            dpre = (inner_rows(weight_ref[...], draw) * slope_ref[:, start:stop]).astype(
                jnp.bfloat16
            )
            second.append(
                jnp.dot(hidden_ref[:, start:stop], draw, preferred_element_type=jnp.float32)
            )
            first.append(
                jnp.dot(dpre, feat_rows(start, stop), preferred_element_type=jnp.float32)
            )
            tile.append(part)
        first_ref[...] = sum(first).T
        second_ref[...] = sum(second)
        tile_ref[...] = sum(tile)
        last = [feat_rows(start, stop) for start, stop in zip(last_starts, last_stops)]
        last_ref[...] = jnp.concatenate(last, axis=0).T

    count = sum(stop - start for start, stop in zip(last_starts, last_stops))
    return pl.pallas_call(
        kernel,
        out_shape=(
            jax.ShapeDtypeStruct((depth, units), jnp.float32),
            jax.ShapeDtypeStruct((units, width), jnp.float32),
            jax.ShapeDtypeStruct((8, lanes), jnp.float32),
            jax.ShapeDtypeStruct((depth, count), jnp.bfloat16),
        ),
        in_specs=in_vmem(len(packed) + len(feats) + 3),
        out_specs=in_vmem(4),
        compiler_params=pltpu.CompilerParams(vmem_limit_bytes=16 << 20),
        name="first_grads",
    )(*packed, *feats, hidden_t, slope_t, weight)


def last_grads(packed, starts, sums, hidden_t, slope_t, weight, rows, total):
    units, width, depth = hidden_t.shape[0], weight.shape[1], sums[0].shape[0]

    def kernel(*refs):
        packed_refs = refs[: len(packed)]
        hidden_ref, slope_ref, weight_ref, first_ref, second_ref, tile_ref, feats_ref = refs[
            len(packed) : -3
        ]
        loss_out, first_out, second_out = refs[-3:]
        draws, tiles = zip(*(unpacked(ref, rows, width) for ref in packed_refs))
        draw = jnp.concatenate(draws, axis=0)
        columns = [
            slice(start, start + values.shape[0]) for start, values in zip(starts, draws)
        ]
        slope = jnp.concatenate([slope_ref[:, part] for part in columns], axis=1)
        hidden = jnp.concatenate([hidden_ref[:, part] for part in columns], axis=1)
        dpre = (inner_rows(weight_ref[...], draw) * slope).astype(jnp.bfloat16)
        first_out[...] = first_ref[...] + inner_rows(feats_ref[...], dpre)
        second_out[...] = second_ref[...] + jnp.dot(
            hidden, draw, preferred_element_type=jnp.float32
        )
        loss_out[0, 0] = jnp.sum(tile_ref[...] + sum(tiles)) / total

    return pl.pallas_call(
        kernel,
        out_shape=(
            jax.ShapeDtypeStruct((1, 1), jnp.float32),
            jax.ShapeDtypeStruct((depth, units), jnp.float32),
            jax.ShapeDtypeStruct((units, width), jnp.float32),
        ),
        in_specs=in_vmem(len(packed) + 7),
        out_specs=[pl.BlockSpec(memory_space=pltpu.SMEM)] + in_vmem(2),
        compiler_params=pltpu.CompilerParams(vmem_limit_bytes=16 << 20),
        name="last_grads",
    )(*packed, hidden_t, slope_t, weight, *sums)


def stage(values):
    def kernel(values_ref, copy_ref):
        copy_ref[...] = values_ref[...]

    return pl.pallas_call(
        kernel,
        out_shape=jax.ShapeDtypeStruct(values.shape, values.dtype),
        in_specs=[pl.BlockSpec(memory_space=pltpu.VMEM)],
        out_specs=pl.BlockSpec(memory_space=pltpu.VMEM),
        compiler_params=pltpu.CompilerParams(vmem_limit_bytes=1 << 20),
        name="stage",
    )(values)


def gelu_exact(values):
    return jax.nn.gelu(values, approximate=False)


def body(clip_feats, teacher_audio, teacher_text, w_first, w_second, pairing):
    rows = clip_feats.shape[0]
    wide_size = lax.axis_size("wide")
    mp_size = lax.axis_size("mp")
    total = rows * wide_size
    part = teacher_text.shape[0]
    half = rows // 2
    wide_bits = bits_down(wide_size)
    mp_bits = bits_down(mp_size)
    own_start = lax.axis_index("mp") % 2 * half

    far_bits, near_bit = wide_bits[:-1], wide_bits[-1]
    far_steps = [("wide", bit) for bit in far_bits]
    gathers = len(far_bits) > 1 and gathers_rows(total, clip_feats.shape[1])

    block = jnp.concatenate(spread(teacher_text, far_steps), axis=0)
    across = swap(block, "wide", near_bit)
    beside = swap(block, "mp", mp_bits[0])
    corner = swap(across, "mp", mp_bits[0])
    most = jnp.concatenate([unit_rows(block), unit_rows(beside), unit_rows(across)], axis=0)
    corner = unit_rows(corner)
    capt_all = jnp.concatenate([most, corner, swap(most, "mp", 1), swap(corner, "mp", 1)], axis=0)
    places = [("wide", bit) for bit in far_bits]
    places += [("mp", mp_bits[0]), ("wide", near_bit), ("mp", 1)]

    pre_act = jnp.dot(clip_feats, w_first, preferred_element_type=jnp.float32)
    hidden = gelu_exact(pre_act).astype(jnp.bfloat16)
    raw = jnp.dot(hidden, w_second, preferred_element_type=jnp.float32)
    own = own_half(raw, own_start, half)
    raw = own + swap(own_half(raw, half - own_start, half), "mp", 1)
    raw = raw + swap(raw, "mp", mp_bits[0])
    teach_b = unit_rows(own_half(teacher_audio, own_start, half))

    place = places_of(own_half(pairing, own_start, half), part, places)

    if not gathers:
        return summed_grads(
            clip_feats, own_start, hidden, pre_act, raw, teach_b, capt_all, place, w_second, total
        )

    draw = loss_step(raw, teach_b, capt_all, place, total)
    sent, masks = [0], [0]
    for bit in far_bits:
        sent += [mask ^ bit for mask in sent]
    for bit in reversed(far_bits):
        masks += [mask ^ bit for mask in masks]
    draws = {0: draw}
    for mask in sent[1:]:
        draws[mask] = swap(draw, "wide", mask)
    middle = len(masks) // 2
    prior = jnp.concatenate([draws[mask] for mask in masks[:middle]], axis=0)
    fresh = jnp.concatenate([draws[mask] for mask in masks[middle:]], axis=0)
    across = swap(prior, "wide", near_bit)
    last = swap(fresh, "wide", near_bit)
    most = jnp.concatenate([prior, fresh, across], axis=0)
    most = [most, swap(most, "mp", 1)]
    rest = rows_of(last, draw, half)
    last = [last, swap(last, "mp", 1)]

    near = own_half(clip_feats, own_start, half)
    near, moved = spread(near, [("wide", bit) for bit in reversed(far_bits)])
    pairs = [
        (near, moved),
        (swap(near, "wide", near_bit), swap(moved, "wide", near_bit)),
    ]
    pairs = [lax.optimization_barrier((*pair, draws[masks[1]]))[:2] for pair in pairs]
    feats = [jnp.concatenate(pair, axis=0) for pair in pairs]
    feats.append(swap(jnp.concatenate(feats, axis=0), "mp", 1))

    pre_t = jnp.concatenate(
        [
            lax.dot_general(
                w_first, rows, (((0,), (1,)), ((), ())), preferred_element_type=jnp.float32
            )
            for rows in feats
        ],
        axis=1,
    )
    gelu_t, gelu_back = jax.vjp(gelu_exact, pre_t)
    slope_t = gelu_back(jnp.ones_like(pre_t))[0]
    hidden_t = gelu_t.astype(jnp.bfloat16)
    factors = (hidden_t, slope_t, stage(w_second))
    starts = [0, total // 2]
    last_starts = [total // 2 - rest, total - rest]
    sums = first_grads(most, starts, last_starts, feats, *factors, half)
    loss, grad_first, grad_second = last_grads(last, last_starts, sums, *factors, half, total)
    return (loss[0, 0], grad_first, grad_second)


def rows_of(packed, block, half):
    return packed.shape[0] // block.shape[0] * half


def places_of(pair, part, places):
    mp_size = lax.axis_size("mp")
    differs = {
        "wide": (pair // (part * mp_size)) ^ lax.axis_index("wide"),
        "mp": (pair // part % mp_size) ^ lax.axis_index("mp"),
    }
    place = pair % part
    for index, (axis, bit) in enumerate(places):
        place = place + (part << index) * (differs[axis] // bit % 2)
    return place[:, None]


def summed_grads(
    clip_feats, own_start, hidden, pre_act, raw, teach_b, capt_all, place, w_second, total
):
    half = raw.shape[0]
    gelu_back = jax.vjp(gelu_exact, pre_act)[1]
    norm = jnp.sqrt(jnp.sum(raw * raw, axis=1, keepdims=True) + eps)
    student = raw / norm
    stud_b = student.astype(jnp.bfloat16)
    scores = inner_rows(jnp.concatenate([teach_b, stud_b], axis=0), capt_all)
    tlog = teacher_scale * scores[:half]
    slog = student_scale * scores[half:]
    hit = jnp.arange(total, dtype=jnp.int32)[None, :] == place
    texp = jnp.exp(tlog)
    sexp = jnp.exp(slog)
    zt_sum = jnp.sum(texp, axis=1)
    zs_sum = jnp.sum(sexp, axis=1)
    acc_sum = jnp.sum(texp * (tlog - slog), axis=1)
    spair = jnp.sum(jnp.where(hit, slog, 0.0), axis=1)
    loss = jnp.sum(acc_sum / zt_sum - jnp.log(zt_sum) + 2.0 * jnp.log(zs_sum) - spair)
    coef = (
        2.0 * sexp / zs_sum[:, None] - texp / zt_sum[:, None] - hit.astype(jnp.float32)
    ).astype(jnp.bfloat16)
    dstud = jnp.dot(coef, capt_all, preferred_element_type=jnp.float32) * (student_scale / total)
    draw = ((dstud - student * jnp.sum(student * dstud, axis=1, keepdims=True)) / norm).astype(
        jnp.bfloat16
    )

    draw = jnp.concatenate([draw, swap(draw, "mp", 1)], axis=0)
    draw = jnp.where(own_start > 0, jnp.roll(draw, half, axis=0), draw)
    grad_second = inner_cols(hidden, draw)
    dpre = gelu_back(inner_rows(draw, w_second))[0].astype(jnp.bfloat16)
    grad_first = inner_cols(clip_feats, dpre)
    tile = jnp.full((8, 128), loss, jnp.float32)
    loss = (tile + swap(tile, "mp", 1))[0, 0]
    grad_first, grad_second, loss = lax.psum((grad_first, grad_second, loss), "wide")
    return (loss / total, grad_first, grad_second)


def gathers_rows(total, depth):
    return 2 * total * depth <= gather_bytes


def solution(mesh):
    return jax.shard_map(
        body,
        mesh=mesh,
        in_specs=(
            P("wide", None),
            P("wide", None),
            P(("wide", "mp"), None),
            P(None, "mp"),
            P("mp", None),
            P("wide"),
        ),
        out_specs=(P(), P(None, "mp"), P("mp", None)),
        check_vma=False,
    )
```
